128 devices in a mesh: pass: 8 (over y_hi, x), red: 8 (over z, core), grp: 2 (over y_lo).
Axes of the slice: x: 4, y: 4 (y_hi: 2, y_lo: 2; y = y_hi * 2 + y_lo), z: 4, core: 2. Of those that a mesh axis runs over, the one named last changes fastest.
Arguments:
- query_lex: bfloat16 [1536, 16384], P(None, 'red')
- query_dense: bfloat16 [1536, 4096], P(None, 'red')
- passage_lex: bfloat16 [8192, 16384], P(('pass', 'grp'), 'red'), may hold values from 0 to 0.47
- passage_dense: bfloat16 [8192, 4096], P(('pass', 'grp'), 'red'), may hold values from -1.33 to 1.33
- positives: int32 [1536], replicated, may hold values from 0 to 8191
Outputs:
- loss_rows: float32 [1536], P('red')
- grad_query_lex: float32 [1536, 16384], P(('pass', 'grp'), 'red')
- grad_query_dense: float32 [1536, 4096], P(('pass', 'grp'), 'red')
- grad_passage_lex: float32 [8192, 16384], P(('pass', 'grp'), 'red')
- grad_passage_dense: float32 [8192, 4096], P(('pass', 'grp'), 'red')
The draws below stay inside these ranges and needn't reach their ends.
All inputs are finite; a program needn't handle non-finite values.
Results may differ from the reference program's by a relative error of at most 0.0022.
Values may be sent and summed in bfloat16 or wider, within the bound.
No kernel may reach another device: no remote copies, remote signals or barrier semaphores. Data moves between devices by JAX's collectives and lax.ppermute only.
A program may use at most 128 MiB of HBM per device.

```python
import jax
import jax.numpy as jnp
from jax import lax

VOCAB = 16384
WIDTH = 4096
QUERIES = 1536
PASSAGES = 8192


lex_scale = 0.46


dense_scale = 0.177


def lexical_row(base, index):
    row_key = jax.random.fold_in(base, index)
    mask_key, value_key = jax.random.split(row_key)
    present = jax.random.bernoulli(mask_key, 0.25, (VOCAB,)).astype(jnp.float32)
    values = jax.random.uniform(value_key, (VOCAB,), jnp.float32)
    ramp = 1.0 + 0.02 * index.astype(jnp.float32) / PASSAGES
    return present * values * lex_scale * ramp


def dense_row(base, index):
    row_key = jax.random.fold_in(base, index)
    value_key = jax.random.fold_in(row_key, 0)
    ramp = 0.75 + 0.5 * index.astype(jnp.float32) / PASSAGES
    values = jnp.clip(jax.random.normal(value_key, (WIDTH,), jnp.float32), -6.0, 6.0)
    return values * dense_scale * ramp


def draw_passage_lex(key, part):
    base = jax.random.fold_in(key, 11)
    indices = jnp.arange(PASSAGES)
    return jax.vmap(lambda index: lexical_row(base, index))(indices).astype(jnp.bfloat16)


def draw_passage_dense(key, part):
    base = jax.random.fold_in(key, 12)
    indices = jnp.arange(PASSAGES)
    return jax.vmap(lambda index: dense_row(base, index))(indices).astype(jnp.bfloat16)


def draw_query_lex(key, part):
    base = jax.random.fold_in(key, 21)
    mask_key, value_key = jax.random.split(base, 2)
    present = jax.random.bernoulli(mask_key, 0.25, (QUERIES, VOCAB)).astype(jnp.float32)
    values = jax.random.uniform(value_key, (QUERIES, VOCAB), jnp.float32)
    drawn = present * values * lex_scale
    return drawn.astype(jnp.bfloat16)


def draw_query_dense(key, part):
    base = jax.random.fold_in(key, 22)
    value_key = jax.random.fold_in(base, 0)
    drawn = jnp.clip(jax.random.normal(value_key, (QUERIES, WIDTH), jnp.float32), -6.0, 6.0) * dense_scale
    return drawn.astype(jnp.bfloat16)


def place_ends(values, own_key, smallest, high):
    longest = values.shape.index(max(values.shape))
    spots = []
    for shift in (0, 1):
        where = [jax.random.randint(jax.random.fold_in(own_key, axis), (), 0, length) for axis, length in enumerate(values.shape)]
        where[longest] = (where[longest] + shift) % values.shape[longest]
        spots.append(tuple(where))
    return values.at[spots[0]].set(smallest).at[spots[1]].set(high)


def setup_inputs(seed: int = 0) -> dict:
    splits = jax.random.split(jax.random.key(seed), 6)
    return {
        "query_lex": draw_query_lex(jax.random.fold_in(splits[5], 71), 0),
        "query_dense": draw_query_dense(jax.random.fold_in(splits[5], 71), 0),
        "passage_lex": draw_passage_lex(jax.random.fold_in(splits[5], 71), 0),
        "passage_dense": draw_passage_dense(jax.random.fold_in(splits[5], 71), 0),
        "positives": place_ends(jax.random.randint(splits[4], (QUERIES,), 0, PASSAGES), jax.random.fold_in(splits[4], 1), 0, PASSAGES - 1).astype(jnp.int32),
    }


def softmax_parts(logits):
    largest = jnp.max(logits, axis=1, keepdims=True)
    total = jnp.sum(jnp.exp(logits - largest), axis=1, keepdims=True)
    log_total = largest + jnp.log(total)
    return log_total[:, 0], jnp.exp(logits - log_total)


def reference(query_lex, query_dense, passage_lex, passage_dense, positives):
    lexical = jnp.dot(query_lex, passage_lex.T, preferred_element_type=jnp.float32)
    dense = jnp.dot(query_dense, passage_dense.T, preferred_element_type=jnp.float32)
    joined = dense + 0.3 * lexical
    columns = lax.broadcasted_iota(jnp.int32, (1, lexical.shape[1]), 1)
    target = (positives.astype(jnp.int32)[:, None] == columns).astype(jnp.float32)
    lse_joined, prob_joined = softmax_parts(joined)
    lse_dense, prob_dense = softmax_parts(dense)
    lse_lexical, prob_lexical = softmax_parts(lexical)
    pick_joined = jnp.sum(target * joined, axis=1)
    pick_dense = jnp.sum(target * dense, axis=1)
    pick_lexical = jnp.sum(target * lexical, axis=1)
    kl_dense = jnp.sum(prob_joined * (joined - dense), axis=1) - lse_joined + lse_dense
    kl_lex = jnp.sum(prob_joined * (joined - lexical), axis=1) - lse_joined + lse_lexical
    loss_rows = (lse_joined - pick_joined) + 0.5 * (lse_dense - pick_dense) + 0.5 * (lse_lexical - pick_lexical) + 0.5 * kl_dense + 0.5 * kl_lex
    grad_dense = (0.5 * prob_joined + prob_dense - 1.5 * target).astype(jnp.bfloat16)
    grad_lex = (-0.2 * prob_joined + prob_lexical - 0.8 * target).astype(jnp.bfloat16)
    grad_query_lex = jnp.dot(grad_lex, passage_lex, preferred_element_type=jnp.float32)
    grad_query_dense = jnp.dot(grad_dense, passage_dense, preferred_element_type=jnp.float32)
    grad_passage_lex = jnp.dot(grad_lex.T, query_lex, preferred_element_type=jnp.float32)
    grad_passage_dense = jnp.dot(grad_dense.T, query_dense, preferred_element_type=jnp.float32)
    return loss_rows, grad_query_lex, grad_query_dense, grad_passage_lex, grad_passage_dense
```

```python
import jax
import jax.numpy as jnp
from jax import lax
from jax.experimental import pallas as pl
from jax.experimental.pallas import tpu as pltpu
from jax.sharding import Mesh, PartitionSpec as P

RED = ("z", "core")
PLANE = ("yh", "x", "yl")
COLUMN = ("yh", "yl")
NT = (((1,), (1,)), ((), ()))
TN = (((0,), (0,)), ((), ()))
NN = (((1,), (0,)), ((), ()))


def matmul(first, second, dims):
    return lax.dot_general(first, second, dims, preferred_element_type=jnp.float32)


def half_scores(half, query_lex, query_dense, passage_lex, passage_dense):
    queries, terms = query_lex.shape
    passages, width = passage_dense.shape
    rows = queries // 8
    part = rows // 4

    def body(half_ref, ql, qd, pl_, pd, out):
        dense = matmul(qd[...], pd[...], NT)
        lexical = matmul(ql[...], pl_[...], NT)
        for x in range(2):
            own = slice(x * rows, (x + 1) * rows)
            out[:, x, :, :passages] = dense[own].reshape(4, part, passages)
            out[:, x, :, passages:] = lexical[own].reshape(4, part, passages)

    return pl.pallas_call(
        body,
        out_shape=jax.ShapeDtypeStruct((4, 4, part, 2 * passages), jnp.float32),
        grid_spec=pltpu.PrefetchScalarGridSpec(
            num_scalar_prefetch=1,
            grid=(2,),
            in_specs=[
                pl.BlockSpec((2 * rows, terms), lambda i, h: (h[0] * 2 + i, 0)),
                pl.BlockSpec((2 * rows, width), lambda i, h: (h[0] * 2 + i, 0)),
                pl.BlockSpec((passages, terms), lambda i, h: (0, 0)),
                pl.BlockSpec((passages, width), lambda i, h: (0, 0)),
            ],
            out_specs=pl.BlockSpec((4, 2, part, 2 * passages), lambda i, h: (0, i, 0, 0)),
        ),
        name="half_scores",
    )(half, query_lex, query_dense, passage_lex, passage_dense)


def query_gradients(place, grads, passage_lex, passage_dense):
    part, passages = grads.shape[3], grads.shape[4] // 2
    terms, width = passage_lex.shape[2], passage_dense.shape[2]
    tiles = terms // width
    rows, own_rows = 8 * part, 2 * part

    def body(place_ref, g, lex, dense, out, own, left, sums):
        step = pl.program_id(0)

        def arrange(low):
            for c in range(2):
                for x in range(4):
                    left[
                        c * 4 * part : (c + 1) * 4 * part, x * passages : (x + 1) * passages
                    ] = g[:, c, x, :, low : low + passages].reshape(4 * part, passages)

        @pl.when(step == 0)
        def _():
            arrange(passages)

        @pl.when(step == tiles)
        def _():
            arrange(0)

        def total(passage):
            sums[...] = matmul(left[...], passage[...].reshape(4 * passages, width), NN)
            out[...] = sums[...].astype(out.dtype)
            at = pl.multiple_of(place_ref[0] * own_rows, own_rows)
            own[...] = sums[pl.ds(at, own_rows), :]

        @pl.when(step < tiles)
        def _():
            total(lex)

        @pl.when(step == tiles)
        def _():
            total(dense)

    return pl.pallas_call(
        body,
        out_shape=(
            jax.ShapeDtypeStruct((rows, terms + width), jnp.bfloat16),
            jax.ShapeDtypeStruct((own_rows, terms + width), jnp.float32),
        ),
        grid_spec=pltpu.PrefetchScalarGridSpec(
            num_scalar_prefetch=1,
            grid=(tiles + 1,),
            in_specs=[
                pl.BlockSpec(grads.shape, lambda i, h: (0, 0, 0, 0, 0)),
                pl.BlockSpec(
                    (4, passages, width), lambda i, h: (0, 0, jnp.minimum(i, tiles - 1))
                ),
                pl.BlockSpec((4, passages, width), lambda i, h: (0, 0, 0)),
            ],
            out_specs=(
                pl.BlockSpec((rows, width), lambda i, h: (0, i)),
                pl.BlockSpec((own_rows, width), lambda i, h: (0, i)),
            ),
            scratch_shapes=[
                pltpu.VMEM((rows, 4 * passages), jnp.bfloat16),
                pltpu.VMEM((rows, width), jnp.float32),
            ],
        ),
        name="query_gradients",
    )(place, grads, passage_lex, passage_dense)


def passage_gradients(grads, query_lex, query_dense):
    part, passages = grads.shape[3], grads.shape[4] // 2
    queries, terms = query_lex.shape
    width = query_dense.shape[1]
    tiles = terms // width

    def body(g, ql, qd, out_lex, out_dense, left):
        step = pl.program_id(0)

        def arrange(low):
            blocks = [
                g[:, block // 4, block % 4, :, low : low + passages].reshape(4 * part, passages)
                for block in range(8)
            ]
            left[...] = jnp.concatenate(blocks, axis=0).T

        @pl.when(step == 0)
        def _():
            arrange(passages)

        @pl.when(step == tiles)
        def _():
            arrange(0)

        @pl.when(step < tiles)
        def _():
            out_lex[...] = matmul(left[...], ql[...], NN)

        @pl.when(step == tiles)
        def _():
            out_dense[...] = matmul(left[...], qd[...], NN)

    return pl.pallas_call(
        body,
        grid=(tiles + 1,),
        out_shape=(
            jax.ShapeDtypeStruct((passages, terms), jnp.float32),
            jax.ShapeDtypeStruct((passages, width), jnp.float32),
        ),
        in_specs=[
            pl.BlockSpec(grads.shape, lambda i: (0, 0, 0, 0, 0)),
            pl.BlockSpec((queries, width), lambda i: (0, jnp.minimum(i, tiles - 1))),
            pl.BlockSpec((queries, width), lambda i: (0, 0)),
        ],
        out_specs=(
            pl.BlockSpec((passages, width), lambda i: (0, jnp.minimum(i, tiles - 1))),
            pl.BlockSpec((passages, width), lambda i: (0, 0)),
        ),
        scratch_shapes=[pltpu.VMEM((passages, queries), jnp.bfloat16)],
        name="passage_gradients",
    )(grads, query_lex, query_dense)


def on_device(query_lex, query_dense, passage_lex, passage_dense, positives):
    core = lax.axis_index("core")
    zed = lax.axis_index("z")
    queries = query_lex.shape[0]
    local_passages = passage_lex.shape[0]
    rows = queries // 8
    part = rows // 4

    line_lex = lax.all_gather(passage_lex, "x", axis=0)
    line_dense = lax.all_gather(passage_dense, "x", axis=0)

    def scores_of(half):
        return half_scores(
            half.astype(jnp.int32)[None], query_lex, query_dense, passage_lex, passage_dense
        )

    arrived = lax.ppermute(scores_of(1 - core), "core", [(0, 1), (1, 0)])
    both = arrived + scores_of(core)
    pieces = lax.all_to_all(both, "z", 0, 0, tiled=True)
    scores2 = pieces.sum(axis=0).reshape(rows, 2 * local_passages)
    dense = scores2[:, :local_passages]
    lexical = scores2[:, local_passages:]

    mine = lax.dynamic_slice(
        positives.reshape(2, 4, 4, part), (core, 0, zed, 0), (1, 4, 1, part)
    ).reshape(rows)
    first_column = lax.axis_index(PLANE) * local_passages
    columns = first_column + lax.broadcasted_iota(jnp.int32, (1, local_passages), 1)
    target = (mine[:, None] == columns).astype(jnp.float32)
    joined = dense + 0.3 * lexical
    scores = (joined, dense, lexical)
    highest = [jnp.max(s, axis=1) for s in scores]
    powers = [jnp.exp(s - h[:, None]) for s, h in zip(scores, highest)]
    stats = (
        highest
        + [jnp.sum(p, axis=1) for p in powers]
        + [
            jnp.sum(powers[0] * (joined - dense), axis=1),
            jnp.sum(powers[0] * (joined - lexical), axis=1),
        ]
        + [jnp.sum(target * s, axis=1) for s in scores]
    )
    stats = jnp.stack(stats)
    stats = lax.all_to_all(
        jnp.broadcast_to(stats[None], (16, *stats.shape)), PLANE, 0, 0, tiled=True
    )
    top = stats[:, 0:3].max(axis=0)
    factor = jnp.exp(stats[:, 0:3] - top[None])
    totals = (stats[:, 3:6] * factor).sum(axis=0)
    weighted = (stats[:, 6:8] * factor[:, 0:1]).sum(axis=0)
    picked = stats[:, 8:11].sum(axis=0)
    logs = top + jnp.log(totals)
    kl_dense = weighted[0] / totals[0] - logs[0] + logs[1]
    kl_lex = weighted[1] / totals[0] - logs[0] + logs[2]
    loss = (
        logs[0]
        - picked[0]
        + 0.5 * (logs[1] - picked[1])
        + 0.5 * (logs[2] - picked[2])
        + 0.5 * kl_dense
        + 0.5 * kl_lex
    )
    prob = [jnp.exp(s - log[:, None]) for s, log in zip(scores, logs)]
    grads = jnp.concatenate(
        [
            (0.5 * prob[0] + prob[1] - 1.5 * target).astype(jnp.bfloat16),
            (-0.2 * prob[0] + prob[2] - 0.8 * target).astype(jnp.bfloat16),
        ],
        axis=1,
    ).reshape(4, part, 2 * local_passages)

    line_grads = lax.all_to_all(grads, "x", 0, 0, tiled=True)
    line_grads, line_lex, line_dense = lax.optimization_barrier(
        (line_grads, line_lex, line_dense)
    )
    line_grads = lax.all_gather(line_grads, RED, axis=0)
    own_grads = lax.all_gather(grads, RED, axis=0)
    all_loss = lax.all_gather(loss, RED, axis=0)
    shape = (4, 2, 4, part, 2 * local_passages)
    place = lax.axis_index(COLUMN)
    sums, own = query_gradients(
        place.astype(jnp.int32)[None], line_grads.reshape(shape), line_lex, line_dense
    )
    sums = lax.all_to_all(sums.reshape(4, 2 * part, -1), COLUMN, 0, 0, tiled=True)
    passage_lex_out, passage_dense_out = passage_gradients(
        own_grads.reshape(shape), query_lex, query_dense
    )
    others = (jnp.arange(4) != place)[:, None, None]

    def summed(low, high):
        wide = jnp.where(others, sums[:, :, low:high].astype(jnp.float32), 0.0)
        return wide.sum(axis=0) + own[:, low:high]

    terms = passage_lex.shape[1]
    query_lex_out = summed(0, terms)
    query_dense_out = summed(terms, sums.shape[2])
    ordered = all_loss.reshape(4, 2, 4, part).transpose(1, 2, 0, 3).reshape(queries)
    loss_rows = lax.dynamic_slice_in_dim(ordered, lax.axis_index(RED) * rows, rows)
    return loss_rows, query_lex_out, query_dense_out, passage_lex_out, passage_dense_out


def solution(mesh):
    fine = Mesh(mesh.devices.reshape(2, 4, 4, 2, 2), ("yh", "x", "z", "core", "yl"))
    return jax.shard_map(
        on_device,
        mesh=fine,
        in_specs=(P(None, RED), P(None, RED), P(PLANE, RED), P(PLANE, RED), P()),
        out_specs=(P(RED), P(PLANE, RED), P(PLANE, RED), P(PLANE, RED), P(PLANE, RED)),
        check_vma=False,
    )
```

```python
import jax
import jax.numpy as jnp
from jax import lax
from jax.experimental import pallas as pl
from jax.experimental.pallas import tpu as pltpu
from jax.sharding import Mesh, PartitionSpec as P

RED = ("z", "core")
PLANE = ("yh", "x", "yl")
COLUMN = ("yh", "yl")
NT = (((1,), (1,)), ((), ()))
TN = (((0,), (0,)), ((), ()))
NN = (((1,), (0,)), ((), ()))


def matmul(first, second, dims):
    return lax.dot_general(first, second, dims, preferred_element_type=jnp.float32)


def half_scores(half, query_lex, query_dense, passage_lex, passage_dense):
    queries, terms = query_lex.shape
    passages, width = passage_dense.shape
    rows = queries // 8
    part = rows // 4

    def body(half_ref, ql, qd, pl_, pd, out):
        dense = matmul(qd[...], pd[...], NT)
        lexical = matmul(ql[...], pl_[...], NT)
        for x in range(2):
            own = slice(x * rows, (x + 1) * rows)
            out[:, x, :, :passages] = dense[own].reshape(4, part, passages)
            out[:, x, :, passages:] = lexical[own].reshape(4, part, passages)

    return pl.pallas_call(
        body,
        out_shape=jax.ShapeDtypeStruct((4, 4, part, 2 * passages), jnp.float32),
        grid_spec=pltpu.PrefetchScalarGridSpec(
            num_scalar_prefetch=1,
            grid=(2,),
            in_specs=[
                pl.BlockSpec((2 * rows, terms), lambda i, h: (h[0] * 2 + i, 0)),
                pl.BlockSpec((2 * rows, width), lambda i, h: (h[0] * 2 + i, 0)),
                pl.BlockSpec((passages, terms), lambda i, h: (0, 0)),
                pl.BlockSpec((passages, width), lambda i, h: (0, 0)),
            ],
            out_specs=pl.BlockSpec((4, 2, part, 2 * passages), lambda i, h: (0, i, 0, 0)),
        ),
        name="half_scores",
    )(half, query_lex, query_dense, passage_lex, passage_dense)


def query_gradients(place, grads, partner, passage_lex, passage_dense):
    part, passages = grads.shape[2], grads.shape[3] // 2
    terms, width = passage_lex.shape[2], passage_dense[0].shape[1]
    tiles = terms // width
    rows, own_rows = 8 * part, 2 * part

    def body(place_ref, g, other, lex, d0, d1, d2, d3, out, own, left, sums):
        dense = (d0, d1, d2, d3)
        step = pl.program_id(0)

        def arrange(low, lines):
            for source, c in ((g, place_ref[1]), (other, 1 - place_ref[1])):
                at = pl.multiple_of(c * 4 * part, 4 * part)
                for x in range(4):
                    left[pl.ds(at, 4 * part), x * passages : (x + 1) * passages] = source[
                        :, lines[x], :, low : low + passages
                    ].reshape(4 * part, passages)

        @pl.when(step == 0)
        def _():
            arrange(passages, range(4))

        def finish():
            out[...] = sums[...].astype(out.dtype)
            at = pl.multiple_of(place_ref[0] * own_rows, own_rows)
            own[...] = sums[pl.ds(at, own_rows), :]

        @pl.when(step < tiles)
        def _():
            sums[...] = matmul(left[...], lex[...].reshape(4 * passages, width), NN)
            finish()

        @pl.when(step == tiles)
        def _():
            arrange(0, [place_ref[2 + x] for x in range(4)])
            acc = None
            for x in range(4):
                at = slice(x * passages, (x + 1) * passages)
                term = matmul(left[:, at], dense[x][...], NN)
                acc = term if acc is None else acc + term
            sums[...] = acc
            finish()

    return pl.pallas_call(
        body,
        out_shape=(
            jax.ShapeDtypeStruct((rows, terms + width), jnp.bfloat16),
            jax.ShapeDtypeStruct((own_rows, terms + width), jnp.float32),
        ),
        grid_spec=pltpu.PrefetchScalarGridSpec(
            num_scalar_prefetch=1,
            grid=(tiles + 1,),
            in_specs=[
                pl.BlockSpec(grads.shape, lambda i, h: (0, 0, 0, 0)),
                pl.BlockSpec(grads.shape, lambda i, h: (0, 0, 0, 0)),
                pl.BlockSpec(
                    (4, passages, width), lambda i, h: (0, 0, jnp.minimum(i, tiles - 1))
                ),
            ]
            + [pl.BlockSpec((passages, width), lambda i, h: (0, 0))] * 4,
            out_specs=(
                pl.BlockSpec((rows, width), lambda i, h: (0, i)),
                pl.BlockSpec((own_rows, width), lambda i, h: (0, i)),
            ),
            scratch_shapes=[
                pltpu.VMEM((rows, 4 * passages), jnp.bfloat16),
                pltpu.VMEM((rows, width), jnp.float32),
            ],
        ),
        name="query_gradients",
    )(place, grads, partner, passage_lex, *passage_dense)


def passage_gradients(grads, query_lex, query_dense):
    part, passages = grads.shape[3], grads.shape[4] // 2
    queries, terms = query_lex.shape
    width = query_dense.shape[1]
    tiles = terms // width

    def body(g, ql, qd, out_lex, out_dense, left):
        step = pl.program_id(0)

        def arrange(low):
            blocks = [
                g[:, block // 4, block % 4, :, low : low + passages].reshape(4 * part, passages)
                for block in range(8)
            ]
            left[...] = jnp.concatenate(blocks, axis=0).T

        @pl.when(step == 0)
        def _():
            arrange(passages)

        @pl.when(step == tiles)
        def _():
            arrange(0)

        @pl.when(step < tiles)
        def _():
            out_lex[...] = matmul(left[...], ql[...], NN)

        @pl.when(step == tiles)
        def _():
            out_dense[...] = matmul(left[...], qd[...], NN)

    return pl.pallas_call(
        body,
        grid=(tiles + 1,),
        out_shape=(
            jax.ShapeDtypeStruct((passages, terms), jnp.float32),
            jax.ShapeDtypeStruct((passages, width), jnp.float32),
        ),
        in_specs=[
            pl.BlockSpec(grads.shape, lambda i: (0, 0, 0, 0, 0)),
            pl.BlockSpec((queries, width), lambda i: (0, jnp.minimum(i, tiles - 1))),
            pl.BlockSpec((queries, width), lambda i: (0, 0)),
        ],
        out_specs=(
            pl.BlockSpec((passages, width), lambda i: (0, jnp.minimum(i, tiles - 1))),
            pl.BlockSpec((passages, width), lambda i: (0, 0)),
        ),
        scratch_shapes=[pltpu.VMEM((passages, queries), jnp.bfloat16)],
        name="passage_gradients",
    )(grads, query_lex, query_dense)


def to_line(value, axis):
    return lax.all_to_all(
        jnp.broadcast_to(value[None], (4, *value.shape)), axis, 0, 0, tiled=True
    )


def on_device(query_lex, query_dense, passage_lex, passage_dense, positives):
    core = lax.axis_index("core")
    zed = lax.axis_index("z")
    ex = lax.axis_index("x")
    queries = query_lex.shape[0]
    local_passages = passage_lex.shape[0]
    rows = queries // 8
    part = rows // 4

    line_lex = lax.all_gather(passage_lex, "x", axis=0)
    def scores_of(half):
        return half_scores(
            half.astype(jnp.int32)[None], query_lex, query_dense, passage_lex, passage_dense
        )

    arrived = lax.ppermute(scores_of(1 - core), "core", [(0, 1), (1, 0)])
    both = arrived + scores_of(core)
    both, passage_later = lax.optimization_barrier((both, passage_dense))
    pieces = lax.all_to_all(both, "z", 0, 0, tiled=True)
    line_dense = [passage_later] + [
        lax.ppermute(passage_later, "x", [(x, (x + k) % 4) for x in range(4)]) for k in (1, 3, 2)
    ]
    pieces, line_dense = lax.optimization_barrier((pieces, line_dense))
    scores2 = pieces.sum(axis=0).reshape(rows, 2 * local_passages)
    dense = scores2[:, :local_passages]
    lexical = scores2[:, local_passages:]

    mine = lax.dynamic_slice(
        positives.reshape(2, 4, 4, part), (core, 0, zed, 0), (1, 4, 1, part)
    ).reshape(rows)
    first_column = lax.axis_index(PLANE) * local_passages
    columns = first_column + lax.broadcasted_iota(jnp.int32, (1, local_passages), 1)
    target = (mine[:, None] == columns).astype(jnp.float32)
    joined = dense + 0.3 * lexical
    scores = (joined, dense, lexical)
    highest = [jnp.max(s, axis=1) for s in scores]
    powers = [jnp.exp(s - h[:, None]) for s, h in zip(scores, highest)]
    stats = (
        highest
        + [jnp.sum(p, axis=1) for p in powers]
        + [
            jnp.sum(powers[0] * (joined - dense), axis=1),
            jnp.sum(powers[0] * (joined - lexical), axis=1),
        ]
        + [jnp.sum(target * s, axis=1) for s in scores]
    )
    stats = jnp.stack(stats)
    stats = lax.all_to_all(
        jnp.broadcast_to(stats[None], (16, *stats.shape)), PLANE, 0, 0, tiled=True
    )
    top = stats[:, 0:3].max(axis=0)
    factor = jnp.exp(stats[:, 0:3] - top[None])
    totals = (stats[:, 3:6] * factor).sum(axis=0)
    weighted = (stats[:, 6:8] * factor[:, 0:1]).sum(axis=0)
    picked = stats[:, 8:11].sum(axis=0)
    logs = top + jnp.log(totals)
    kl_dense = weighted[0] / totals[0] - logs[0] + logs[1]
    kl_lex = weighted[1] / totals[0] - logs[0] + logs[2]
    loss = (
        logs[0]
        - picked[0]
        + 0.5 * (logs[1] - picked[1])
        + 0.5 * (logs[2] - picked[2])
        + 0.5 * kl_dense
        + 0.5 * kl_lex
    )
    prob = [jnp.exp(s - log[:, None]) for s, log in zip(scores, logs)]
    grads = jnp.concatenate(
        [
            (0.5 * prob[0] + prob[1] - 1.5 * target).astype(jnp.bfloat16),
            (-0.2 * prob[0] + prob[2] - 0.8 * target).astype(jnp.bfloat16),
        ],
        axis=1,
    ).reshape(4, part, 2 * local_passages)

    line_grads = lax.all_to_all(grads, "x", 0, 0, tiled=True)
    line_grads = to_line(line_grads, "z")
    partner_grads = lax.ppermute(line_grads, "core", [(0, 1), (1, 0)])
    partner_grads, grads = lax.optimization_barrier((partner_grads, grads))
    own_grads = lax.all_gather(grads, RED, axis=0)
    all_loss = lax.all_gather(loss, RED, axis=0)
    shape = (4, 2, 4, part, 2 * local_passages)
    place = lax.axis_index(COLUMN)
    sums, own = query_gradients(
        jnp.stack([place, core, ex, (ex + 3) % 4, (ex + 1) % 4, (ex + 2) % 4]).astype(jnp.int32),
        line_grads,
        partner_grads,
        line_lex,
        line_dense,
    )
    sums = lax.all_to_all(sums.reshape(4, 2 * part, -1), COLUMN, 0, 0, tiled=True)
    passage_lex_out, passage_dense_out = passage_gradients(
        own_grads.reshape(shape), query_lex, query_dense
    )
    others = (jnp.arange(4) != place)[:, None, None]

    def summed(low, high):
        wide = jnp.where(others, sums[:, :, low:high].astype(jnp.float32), 0.0)
        return wide.sum(axis=0) + own[:, low:high]

    terms = passage_lex.shape[1]
    query_lex_out = summed(0, terms)
    query_dense_out = summed(terms, sums.shape[2])
    ordered = all_loss.reshape(4, 2, 4, part).transpose(1, 2, 0, 3).reshape(queries)
    loss_rows = lax.dynamic_slice_in_dim(ordered, lax.axis_index(RED) * rows, rows)
    return loss_rows, query_lex_out, query_dense_out, passage_lex_out, passage_dense_out


def solution(mesh):
    fine = Mesh(mesh.devices.reshape(2, 4, 4, 2, 2), ("yh", "x", "z", "core", "yl"))
    return jax.shard_map(
        on_device,
        mesh=fine,
        in_specs=(P(None, RED), P(None, RED), P(PLANE, RED), P(PLANE, RED), P()),
        out_specs=(P(RED), P(PLANE, RED), P(PLANE, RED), P(PLANE, RED), P(PLANE, RED)),
        check_vma=False,
    )
```

```python
import jax
import jax.numpy as jnp
from jax import lax
from jax.experimental import pallas as pl
from jax.experimental.pallas import tpu as pltpu
from jax.sharding import Mesh, PartitionSpec as P

RED = ("z", "core")
PLANE = ("yh", "x", "yl")
COLUMN = ("yh", "yl")
NT = (((1,), (1,)), ((), ()))
NN = (((1,), (0,)), ((), ()))


def matmul(first, second, dims):
    return lax.dot_general(first, second, dims, preferred_element_type=jnp.float32)


def half_scores(half, query_lex, query_dense, passage_lex, passage_dense):
    queries, terms = query_lex.shape
    passages, width = passage_dense.shape
    rows = queries // 8
    part = rows // 4

    def body(half_ref, ql, qd, pl_, pd, out):
        dense = matmul(qd[...], pd[...], NT)
        lexical = matmul(ql[...], pl_[...], NT)
        for x in range(2):
            own = slice(x * rows, (x + 1) * rows)
            out[:, x, :, :passages] = dense[own].reshape(4, part, passages)
            out[:, x, :, passages:] = lexical[own].reshape(4, part, passages)

    return pl.pallas_call(
        body,
        out_shape=jax.ShapeDtypeStruct((4, 4, part, 2 * passages), jnp.float32),
        grid_spec=pltpu.PrefetchScalarGridSpec(
            num_scalar_prefetch=1,
            grid=(2,),
            in_specs=[
                pl.BlockSpec((2 * rows, terms), lambda i, h: (h[0] * 2 + i, 0)),
                pl.BlockSpec((2 * rows, width), lambda i, h: (h[0] * 2 + i, 0)),
                pl.BlockSpec((passages, terms), lambda i, h: (0, 0)),
                pl.BlockSpec((passages, width), lambda i, h: (0, 0)),
            ],
            out_specs=pl.BlockSpec((4, 2, part, 2 * passages), lambda i, h: (0, i, 0, 0)),
        ),
        name="half_scores",
    )(half, query_lex, query_dense, passage_lex, passage_dense)


def query_gradients(place, grads, partner, passage_lex, passage_dense):
    part, passages = grads.shape[2], grads.shape[3] // 2
    terms, width = passage_lex.shape[2], passage_dense[0].shape[1]
    tiles = terms // width
    rows, own_rows = 8 * part, 2 * part

    def body(place_ref, g, other, lex, d0, d1, d2, d3, out, own, left, sums):
        dense = (d0, d1, d2, d3)
        step = pl.program_id(0)

        def arrange(low, lines):
            for source, c in ((g, place_ref[1]), (other, 1 - place_ref[1])):
                at = pl.multiple_of(c * 4 * part, 4 * part)
                for x in range(4):
                    left[pl.ds(at, 4 * part), x * passages : (x + 1) * passages] = source[
                        :, lines[x], :, low : low + passages
                    ].reshape(4 * part, passages)

        @pl.when(step == 0)
        def _():
            arrange(passages, [place_ref[2 + x] for x in range(4)])

        def finish():
            out[...] = sums[...].astype(out.dtype)
            at = pl.multiple_of(place_ref[0] * own_rows, own_rows)
            own[...] = sums[pl.ds(at, own_rows), :]

        @pl.when(step < tiles)
        def _():
            sums[...] = matmul(left[...], lex[...].reshape(4 * passages, width), NN)
            finish()

        @pl.when(step == tiles)
        def _():
            arrange(0, range(4))
            acc = None
            for x in range(4):
                at = slice(x * passages, (x + 1) * passages)
                term = matmul(left[:, at], dense[x][...], NN)
                acc = term if acc is None else acc + term
            sums[...] = acc
            finish()

    return pl.pallas_call(
        body,
        out_shape=(
            jax.ShapeDtypeStruct((rows, terms + width), jnp.bfloat16),
            jax.ShapeDtypeStruct((own_rows, terms + width), jnp.float32),
        ),
        grid_spec=pltpu.PrefetchScalarGridSpec(
            num_scalar_prefetch=1,
            grid=(tiles + 1,),
            in_specs=[
                pl.BlockSpec(grads.shape, lambda i, h: (0, 0, 0, 0)),
                pl.BlockSpec(grads.shape, lambda i, h: (0, 0, 0, 0)),
                pl.BlockSpec(
                    (4, passages, width), lambda i, h: (0, 0, jnp.minimum(i, tiles - 1))
                ),
            ]
            + [pl.BlockSpec((passages, width), lambda i, h: (0, 0))] * 4,
            out_specs=(
                pl.BlockSpec((rows, width), lambda i, h: (0, i)),
                pl.BlockSpec((own_rows, width), lambda i, h: (0, i)),
            ),
            scratch_shapes=[
                pltpu.VMEM((rows, 4 * passages), jnp.bfloat16),
                pltpu.VMEM((rows, width), jnp.float32),
            ],
        ),
        name="query_gradients",
    )(place, grads, partner, passage_lex, *passage_dense)


def passage_gradients(grads, query_lex, query_dense):
    part, passages = grads.shape[3], grads.shape[4] // 2
    queries, terms = query_lex.shape
    width = query_dense.shape[1]
    tiles = terms // width

    def body(g, ql, qd, out_lex, out_dense, left):
        step = pl.program_id(0)

        def arrange(low):
            blocks = [
                g[:, block // 4, block % 4, :, low : low + passages].reshape(4 * part, passages)
                for block in range(8)
            ]
            left[...] = jnp.concatenate(blocks, axis=0).T

        @pl.when(step == 0)
        def _():
            arrange(passages)

        @pl.when(step == tiles)
        def _():
            arrange(0)

        @pl.when(step < tiles)
        def _():
            out_lex[...] = matmul(left[...], ql[...], NN)

        @pl.when(step == tiles)
        def _():
            out_dense[...] = matmul(left[...], qd[...], NN)

    return pl.pallas_call(
        body,
        grid=(tiles + 1,),
        out_shape=(
            jax.ShapeDtypeStruct((passages, terms), jnp.float32),
            jax.ShapeDtypeStruct((passages, width), jnp.float32),
        ),
        in_specs=[
            pl.BlockSpec(grads.shape, lambda i: (0, 0, 0, 0, 0)),
            pl.BlockSpec((queries, width), lambda i: (0, jnp.minimum(i, tiles - 1))),
            pl.BlockSpec((queries, width), lambda i: (0, 0)),
        ],
        out_specs=(
            pl.BlockSpec((passages, width), lambda i: (0, jnp.minimum(i, tiles - 1))),
            pl.BlockSpec((passages, width), lambda i: (0, 0)),
        ),
        scratch_shapes=[pltpu.VMEM((passages, queries), jnp.bfloat16)],
        name="passage_gradients",
    )(grads, query_lex, query_dense)


def to_line(value, axis):
    return lax.all_to_all(
        jnp.broadcast_to(value[None], (4, *value.shape)), axis, 0, 0, tiled=True
    )


def step(query_lex, query_dense, passage_lex, passage_dense, positives):
    core = lax.axis_index("core")
    zed = lax.axis_index("z")
    ex = lax.axis_index("x")
    queries = query_lex.shape[0]
    local_passages = passage_lex.shape[0]
    rows = queries // 8
    part = rows // 4

    line_lex = lax.all_gather(passage_lex, "x", axis=0)

    def scores_of(half):
        return half_scores(
            half.astype(jnp.int32)[None], query_lex, query_dense, passage_lex, passage_dense
        )

    arrived = lax.ppermute(scores_of(1 - core), "core", [(0, 1), (1, 0)])
    both = arrived + scores_of(core)

    def shifted(value, k):
        return lax.ppermute(value, "x", [(x, (x + k) % 4) for x in range(4)])

    both, passage_later = lax.optimization_barrier((both, passage_dense))
    pieces = lax.all_to_all(both, "z", 0, 0, tiled=True)
    near_dense = [shifted(passage_later, 1), shifted(passage_later, 3)]
    far_dense = shifted(passage_later, 2)
    line_dense = [passage_dense, *near_dense, far_dense]
    scores4 = pieces.sum(axis=0)
    scores2 = scores4.reshape(rows, 2 * local_passages)
    dense = scores2[:, :local_passages]
    lexical = scores2[:, local_passages:]
    line_scores = [lax.dynamic_index_in_dim(scores4, ex, 0, keepdims=False)]
    for k in (1, 3, 2):
        part_scores = lax.dynamic_index_in_dim(scores4, (ex + k) % 4, 0, keepdims=False)
        line_scores.append(shifted(part_scores, k))

    mine = lax.dynamic_slice(
        positives.reshape(2, 4, 4, part), (core, 0, zed, 0), (1, 4, 1, part)
    ).reshape(rows)
    first_column = lax.axis_index(PLANE) * local_passages
    columns = first_column + lax.broadcasted_iota(jnp.int32, (1, local_passages), 1)
    target = (mine[:, None] == columns).astype(jnp.float32)
    joined = dense + 0.3 * lexical
    scores = (joined, dense, lexical)
    highest = [jnp.max(s, axis=1) for s in scores]
    powers = [jnp.exp(s - h[:, None]) for s, h in zip(scores, highest)]
    stats = (
        highest
        + [jnp.sum(p, axis=1) for p in powers]
        + [
            jnp.sum(powers[0] * (joined - dense), axis=1),
            jnp.sum(powers[0] * (joined - lexical), axis=1),
        ]
        + [jnp.sum(target * s, axis=1) for s in scores]
    )
    stats = jnp.stack(stats)
    stats = lax.all_to_all(
        jnp.broadcast_to(stats[None], (16, *stats.shape)), PLANE, 0, 0, tiled=True
    )
    top = stats[:, 0:3].max(axis=0)
    factor = jnp.exp(stats[:, 0:3] - top[None])
    totals = (stats[:, 3:6] * factor).sum(axis=0)
    weighted = (stats[:, 6:8] * factor[:, 0:1]).sum(axis=0)
    picked = stats[:, 8:11].sum(axis=0)
    logs = top + jnp.log(totals)
    kl_dense = weighted[0] / totals[0] - logs[0] + logs[1]
    kl_lex = weighted[1] / totals[0] - logs[0] + logs[2]
    loss = (
        logs[0]
        - picked[0]
        + 0.5 * (logs[1] - picked[1])
        + 0.5 * (logs[2] - picked[2])
        + 0.5 * kl_dense
        + 0.5 * kl_lex
    )

    def gradients(dense, lexical, logs, target):
        joined = dense + 0.3 * lexical
        prob = [jnp.exp(s - log[..., None]) for s, log in zip((joined, dense, lexical), logs)]
        return jnp.concatenate(
            [
                (0.5 * prob[0] + prob[1] - 1.5 * target).astype(jnp.bfloat16),
                (-0.2 * prob[0] + prob[2] - 0.8 * target).astype(jnp.bfloat16),
            ],
            axis=-1,
        )

    grads = gradients(dense, lexical, logs, target).reshape(4, part, 2 * local_passages)
    line_logs = lax.dynamic_index_in_dim(logs.reshape(3, 4, part), ex, 1, keepdims=False)
    line_mine = lax.dynamic_index_in_dim(mine.reshape(4, part), ex, 0, keepdims=False)
    line_grads = []
    for k, both_scores in zip((0, 1, 3, 2), line_scores):
        start = (lax.axis_index("yh") * 4 + (ex + 4 - k) % 4) * 2 + lax.axis_index("yl")
        line_columns = start * local_passages + lax.broadcasted_iota(
            jnp.int32, (1, local_passages), 1
        )
        line_target = (line_mine[:, None] == line_columns).astype(jnp.float32)
        line_grads.append(
            gradients(
                both_scores[:, :local_passages],
                both_scores[:, local_passages:],
                line_logs,
                line_target,
            )
        )
    line_grads = jnp.stack(line_grads)
    line_grads = to_line(line_grads, "z")
    line_grads, grads = lax.optimization_barrier((line_grads, grads))
    partner_grads = lax.ppermute(line_grads, "core", [(0, 1), (1, 0)])
    own_grads = lax.all_gather(grads, RED, axis=0)
    all_loss = lax.all_gather(loss, RED, axis=0)
    shape = (4, 2, 4, part, 2 * local_passages)
    place = lax.axis_index(COLUMN)

    def slot_of(x):
        away = (x + 4 - ex) % 4
        return jnp.where(away == 2, 3, jnp.where(away == 3, 1, away * 2))

    sums, own = query_gradients(
        jnp.stack([place, core] + [slot_of(x) for x in range(4)]).astype(jnp.int32),
        line_grads,
        partner_grads,
        line_lex,
        line_dense,
    )
    sums = lax.all_to_all(sums.reshape(4, 2 * part, -1), COLUMN, 0, 0, tiled=True)
    passage_lex_out, passage_dense_out = passage_gradients(
        own_grads.reshape(shape), query_lex, query_dense
    )
    others = (jnp.arange(4) != place)[:, None, None]

    def summed(low, high):
        wide = jnp.where(others, sums[:, :, low:high].astype(jnp.float32), 0.0)
        return wide.sum(axis=0) + own[:, low:high]

    terms = passage_lex.shape[1]
    query_lex_out = summed(0, terms)
    query_dense_out = summed(terms, sums.shape[2])
    ordered = all_loss.reshape(4, 2, 4, part).transpose(1, 2, 0, 3).reshape(queries)
    loss_rows = lax.dynamic_slice_in_dim(ordered, lax.axis_index(RED) * rows, rows)
    return loss_rows, query_lex_out, query_dense_out, passage_lex_out, passage_dense_out


def solution(mesh):
    fine = Mesh(mesh.devices.reshape(2, 4, 4, 2, 2), ("yh", "x", "z", "core", "yl"))
    return jax.shard_map(
        step,
        mesh=fine,
        in_specs=(P(None, RED), P(None, RED), P(PLANE, RED), P(PLANE, RED), P()),
        out_specs=(P(RED), P(PLANE, RED), P(PLANE, RED), P(PLANE, RED), P(PLANE, RED)),
        check_vma=False,
    )
```

```python
import jax
import jax.numpy as jnp
from jax import lax
from jax.experimental import pallas as pl
from jax.experimental.pallas import tpu as pltpu
from jax.sharding import Mesh, PartitionSpec as P

RED = ("z", "core")
PLANE = ("yh", "x", "yl")
COLUMN = ("yh", "yl")
NT = (((1,), (1,)), ((), ()))
NN = (((1,), (0,)), ((), ()))


def matmul(first, second, dims):
    return lax.dot_general(first, second, dims, preferred_element_type=jnp.float32)


def half_scores(half, query_lex, query_dense, passage_lex, passage_dense):
    queries, terms = query_lex.shape
    passages, width = passage_dense.shape
    rows = queries // 8
    part = rows // 4

    def body(half_ref, ql, qd, pl_, pd, out):
        dense = matmul(qd[...], pd[...], NT)
        lexical = matmul(ql[...], pl_[...], NT)
        for x in range(2):
            own = slice(x * rows, (x + 1) * rows)
            out[:, x, :, :passages] = dense[own].reshape(4, part, passages)
            out[:, x, :, passages:] = lexical[own].reshape(4, part, passages)

    return pl.pallas_call(
        body,
        out_shape=jax.ShapeDtypeStruct((4, 4, part, 2 * passages), jnp.float32),
        grid_spec=pltpu.PrefetchScalarGridSpec(
            num_scalar_prefetch=1,
            grid=(2,),
            in_specs=[
                pl.BlockSpec((2 * rows, terms), lambda i, h: (h[0] * 2 + i, 0)),
                pl.BlockSpec((2 * rows, width), lambda i, h: (h[0] * 2 + i, 0)),
                pl.BlockSpec((passages, terms), lambda i, h: (0, 0)),
                pl.BlockSpec((passages, width), lambda i, h: (0, 0)),
            ],
            out_specs=pl.BlockSpec((4, 2, part, 2 * passages), lambda i, h: (0, i, 0, 0)),
        ),
        name="half_scores",
    )(half, query_lex, query_dense, passage_lex, passage_dense)


def query_gradients(place, grads, partner, passage_lex, passage_dense):
    part, passages = grads.shape[2], grads.shape[3] // 2
    terms, width = passage_lex.shape[2], passage_dense[0].shape[1]
    tiles = terms // width
    rows, own_rows = 8 * part, 2 * part

    def body(place_ref, core_ref, ex_ref, g, other, lex, d0, d1, d2, d3, out, own, left, sums):
        dense = (d0, d1, d2, d3)
        step = pl.program_id(0)

        def slot_of(x):
            away = (x + 4 - ex_ref[0]) % 4
            return jnp.where(away == 2, 3, jnp.where(away == 3, 1, away * 2))

        def arrange(low, lines):
            for source, c in ((g, core_ref[0]), (other, 1 - core_ref[0])):
                at = pl.multiple_of(c * 4 * part, 4 * part)
                for x in range(4):
                    left[pl.ds(at, 4 * part), x * passages : (x + 1) * passages] = source[
                        :, lines[x], :, low : low + passages
                    ].reshape(4 * part, passages)

        @pl.when(step == 0)
        def _():
            arrange(passages, [slot_of(x) for x in range(4)])

        def finish():
            out[...] = sums[...].astype(out.dtype)
            at = pl.multiple_of(place_ref[0] * own_rows, own_rows)
            own[...] = sums[pl.ds(at, own_rows), :]

        @pl.when(step < tiles)
        def _():
            sums[...] = matmul(left[...], lex[...].reshape(4 * passages, width), NN)
            finish()

        @pl.when(step == tiles)
        def _():
            arrange(0, range(4))
            acc = None
            for x in range(4):
                at = slice(x * passages, (x + 1) * passages)
                term = matmul(left[:, at], dense[x][...], NN)
                acc = term if acc is None else acc + term
            sums[...] = acc
            finish()

    return pl.pallas_call(
        body,
        out_shape=(
            jax.ShapeDtypeStruct((rows, terms + width), jnp.bfloat16),
            jax.ShapeDtypeStruct((own_rows, terms + width), jnp.float32),
        ),
        grid_spec=pltpu.PrefetchScalarGridSpec(
            num_scalar_prefetch=3,
            grid=(tiles + 1,),
            in_specs=[
                pl.BlockSpec(grads.shape, lambda i, *h: (0, 0, 0, 0)),
                pl.BlockSpec(grads.shape, lambda i, *h: (0, 0, 0, 0)),
                pl.BlockSpec(
                    (4, passages, width), lambda i, *h: (0, 0, jnp.minimum(i, tiles - 1))
                ),
            ]
            + [pl.BlockSpec((passages, width), lambda i, *h: (0, 0))] * 4,
            out_specs=(
                pl.BlockSpec((rows, width), lambda i, *h: (0, i)),
                pl.BlockSpec((own_rows, width), lambda i, *h: (0, i)),
            ),
            scratch_shapes=[
                pltpu.VMEM((rows, 4 * passages), jnp.bfloat16),
                pltpu.VMEM((rows, width), jnp.float32),
            ],
        ),
        name="query_gradients",
    )(*place, grads, partner, passage_lex, *passage_dense)


def passage_gradients(grads, query_lex, query_dense):
    part, passages = grads.shape[3], grads.shape[4] // 2
    queries, terms = query_lex.shape
    width = query_dense.shape[1]
    tiles = terms // width

    def body(g, ql, qd, out_lex, out_dense, left):
        step = pl.program_id(0)

        def arrange(low):
            blocks = [
                g[:, block // 4, block % 4, :, low : low + passages].reshape(4 * part, passages)
                for block in range(8)
            ]
            left[...] = jnp.concatenate(blocks, axis=0).T

        @pl.when(step == 0)
        def _():
            arrange(passages)

        @pl.when(step == tiles)
        def _():
            arrange(0)

        @pl.when(step < tiles)
        def _():
            out_lex[...] = matmul(left[...], ql[...], NN)

        @pl.when(step == tiles)
        def _():
            out_dense[...] = matmul(left[...], qd[...], NN)

    return pl.pallas_call(
        body,
        grid=(tiles + 1,),
        out_shape=(
            jax.ShapeDtypeStruct((passages, terms), jnp.float32),
            jax.ShapeDtypeStruct((passages, width), jnp.float32),
        ),
        in_specs=[
            pl.BlockSpec(grads.shape, lambda i: (0, 0, 0, 0, 0)),
            pl.BlockSpec((queries, width), lambda i: (0, jnp.minimum(i, tiles - 1))),
            pl.BlockSpec((queries, width), lambda i: (0, 0)),
        ],
        out_specs=(
            pl.BlockSpec((passages, width), lambda i: (0, jnp.minimum(i, tiles - 1))),
            pl.BlockSpec((passages, width), lambda i: (0, 0)),
        ),
        scratch_shapes=[pltpu.VMEM((passages, queries), jnp.bfloat16)],
        name="passage_gradients",
    )(grads, query_lex, query_dense)


def to_line(value, axis):
    return lax.all_to_all(
        jnp.broadcast_to(value[None], (4, *value.shape)), axis, 0, 0, tiled=True
    )


def step(query_lex, query_dense, passage_lex, passage_dense, positives):
    core = lax.axis_index("core")
    zed = lax.axis_index("z")
    ex = lax.axis_index("x")
    queries = query_lex.shape[0]
    local_passages = passage_lex.shape[0]
    rows = queries // 8
    part = rows // 4

    line_lex = lax.all_gather(passage_lex, "x", axis=0)

    def scores_of(half):
        return half_scores(
            half.astype(jnp.int32)[None], query_lex, query_dense, passage_lex, passage_dense
        )

    arrived = lax.ppermute(scores_of(1 - core), "core", [(0, 1), (1, 0)])
    both = arrived + scores_of(core)

    def shifted(value, k):
        return lax.ppermute(value, "x", [(x, (x + k) % 4) for x in range(4)])

    both, passage_later = lax.optimization_barrier((both, passage_dense))
    pieces = lax.all_to_all(both, "z", 0, 0, tiled=True)
    near_dense = [shifted(passage_later, 1), shifted(passage_later, 3)]
    scores4 = pieces.sum(axis=0)
    scores2 = scores4.reshape(rows, 2 * local_passages)
    dense = scores2[:, :local_passages]
    lexical = scores2[:, local_passages:]
    line_scores = [lax.dynamic_index_in_dim(scores4, ex, 0, keepdims=False)]
    for k in (1, 3, 2):
        part_scores = lax.dynamic_index_in_dim(scores4, (ex + k) % 4, 0, keepdims=False)
        line_scores.append(shifted(part_scores, k))

    mine = lax.dynamic_slice(
        positives.reshape(2, 4, 4, part), (core, 0, zed, 0), (1, 4, 1, part)
    ).reshape(rows)
    first_column = lax.axis_index(PLANE) * local_passages
    columns = first_column + lax.broadcasted_iota(jnp.int32, (1, local_passages), 1)
    target = (mine[:, None] == columns).astype(jnp.float32)
    joined = dense + 0.3 * lexical
    scores = (joined, dense, lexical)
    highest = [jnp.max(s, axis=1) for s in scores]
    powers = [jnp.exp(s - h[:, None]) for s, h in zip(scores, highest)]
    stats = (
        highest
        + [jnp.sum(p, axis=1) for p in powers]
        + [
            jnp.sum(powers[0] * (joined - dense), axis=1),
            jnp.sum(powers[0] * (joined - lexical), axis=1),
        ]
        + [jnp.sum(target * s, axis=1) for s in scores]
    )
    stats = jnp.stack(stats)
    stats = lax.all_to_all(
        jnp.broadcast_to(stats[None], (16, *stats.shape)), PLANE, 0, 0, tiled=True
    )
    top = stats[:, 0:3].max(axis=0)
    factor = jnp.exp(stats[:, 0:3] - top[None])
    totals = (stats[:, 3:6] * factor).sum(axis=0)
    weighted = (stats[:, 6:8] * factor[:, 0:1]).sum(axis=0)
    picked = stats[:, 8:11].sum(axis=0)
    logs = top + jnp.log(totals)
    kl_dense = weighted[0] / totals[0] - logs[0] + logs[1]
    kl_lex = weighted[1] / totals[0] - logs[0] + logs[2]
    loss = (
        logs[0]
        - picked[0]
        + 0.5 * (logs[1] - picked[1])
        + 0.5 * (logs[2] - picked[2])
        + 0.5 * kl_dense
        + 0.5 * kl_lex
    )

    def gradients(dense, lexical, logs, target):
        joined = dense + 0.3 * lexical
        prob = [jnp.exp(s - log[..., None]) for s, log in zip((joined, dense, lexical), logs)]
        return jnp.concatenate(
            [
                (0.5 * prob[0] + prob[1] - 1.5 * target).astype(jnp.bfloat16),
                (-0.2 * prob[0] + prob[2] - 0.8 * target).astype(jnp.bfloat16),
            ],
            axis=-1,
        )

    grads = gradients(dense, lexical, logs, target).reshape(4, part, 2 * local_passages)
    line_logs = lax.dynamic_index_in_dim(logs.reshape(3, 4, part), ex, 1, keepdims=False)
    line_mine = lax.dynamic_index_in_dim(mine.reshape(4, part), ex, 0, keepdims=False)
    line_grads = []
    for k, both_scores in zip((0, 1, 3, 2), line_scores):
        start = (lax.axis_index("yh") * 4 + (ex + 4 - k) % 4) * 2 + lax.axis_index("yl")
        line_columns = start * local_passages + lax.broadcasted_iota(
            jnp.int32, (1, local_passages), 1
        )
        line_target = (line_mine[:, None] == line_columns).astype(jnp.float32)
        line_grads.append(
            gradients(
                both_scores[:, :local_passages],
                both_scores[:, local_passages:],
                line_logs,
                line_target,
            )
        )
    line_grads = jnp.stack(line_grads)
    line_grads, passage_far = lax.optimization_barrier((line_grads, passage_dense))
    line_grads = to_line(line_grads, "z")
    far_dense = shifted(passage_far, 2)
    line_dense = [passage_dense, *near_dense, far_dense]
    line_grads, grads = lax.optimization_barrier((line_grads, grads))
    partner_grads = lax.ppermute(line_grads, "core", [(0, 1), (1, 0)])
    own_grads = lax.all_gather(grads, RED, axis=0)
    all_loss = lax.all_gather(loss, RED, axis=0)
    shape = (4, 2, 4, part, 2 * local_passages)
    place = lax.axis_index(COLUMN)

    sums, own = query_gradients(
        [scalar.astype(jnp.int32)[None] for scalar in (place, core, ex)],
        line_grads,
        partner_grads,
        line_lex,
        line_dense,
    )
    sums = lax.all_to_all(sums.reshape(4, 2 * part, -1), COLUMN, 0, 0, tiled=True)
    passage_lex_out, passage_dense_out = passage_gradients(
        own_grads.reshape(shape), query_lex, query_dense
    )
    others = (jnp.arange(4) != place)[:, None, None]

    def summed(low, high):
        wide = jnp.where(others, sums[:, :, low:high].astype(jnp.float32), 0.0)
        return wide.sum(axis=0) + own[:, low:high]

    terms = passage_lex.shape[1]
    query_lex_out = summed(0, terms)
    query_dense_out = summed(terms, sums.shape[2])
    ordered = all_loss.reshape(4, 2, 4, part).transpose(1, 2, 0, 3).reshape(queries)
    loss_rows = lax.dynamic_slice_in_dim(ordered, lax.axis_index(RED) * rows, rows)
    return loss_rows, query_lex_out, query_dense_out, passage_lex_out, passage_dense_out


def solution(mesh):
    fine = Mesh(mesh.devices.reshape(2, 4, 4, 2, 2), ("yh", "x", "z", "core", "yl"))
    return jax.shard_map(
        step,
        mesh=fine,
        in_specs=(P(None, RED), P(None, RED), P(PLANE, RED), P(PLANE, RED), P()),
        out_specs=(P(RED), P(PLANE, RED), P(PLANE, RED), P(PLANE, RED), P(PLANE, RED)),
        check_vma=False,
    )
```

```python
import jax
import jax.numpy as jnp
from jax import lax
from jax.experimental import pallas as pl
from jax.experimental.pallas import tpu as pltpu
from jax.sharding import Mesh, PartitionSpec as P

RED = ("z", "core")
PLANE = ("yh", "x", "yl")
COLUMN = ("yh", "yl")
NT = (((1,), (1,)), ((), ()))
NN = (((1,), (0,)), ((), ()))


def matmul(first, second, dims):
    return lax.dot_general(first, second, dims, preferred_element_type=jnp.float32)


def half_scores(half, query_lex, query_dense, passage_lex, passage_dense):
    queries, terms = query_lex.shape
    passages, width = passage_dense.shape
    rows = queries // 8
    part = rows // 4

    def body(half_ref, ql, qd, pl_, pd, out):
        dense = matmul(qd[...], pd[...], NT)
        lexical = matmul(ql[...], pl_[...], NT)
        for x in range(2):
            own = slice(x * rows, (x + 1) * rows)
            out[:, x, :, :passages] = dense[own].reshape(4, part, passages)
            out[:, x, :, passages:] = lexical[own].reshape(4, part, passages)

    return pl.pallas_call(
        body,
        out_shape=jax.ShapeDtypeStruct((4, 4, part, 2 * passages), jnp.float32),
        grid_spec=pltpu.PrefetchScalarGridSpec(
            num_scalar_prefetch=1,
            grid=(2,),
            in_specs=[
                pl.BlockSpec((2 * rows, terms), lambda i, h: (h[0] * 2 + i, 0)),
                pl.BlockSpec((2 * rows, width), lambda i, h: (h[0] * 2 + i, 0)),
                pl.BlockSpec((passages, terms), lambda i, h: (0, 0)),
                pl.BlockSpec((passages, width), lambda i, h: (0, 0)),
            ],
            out_specs=pl.BlockSpec((4, 2, part, 2 * passages), lambda i, h: (0, i, 0, 0)),
        ),
        name="half_scores",
    )(half, query_lex, query_dense, passage_lex, passage_dense)


def query_gradients(place, grads, partner, passage_lex, passage_dense):
    part, passages = grads.shape[2], grads.shape[3] // 2
    terms, width = passage_lex.shape[2], passage_dense[0].shape[1]
    tiles = terms // width
    rows, own_rows = 8 * part, 2 * part

    def body(place_ref, core_ref, ex_ref, g, other, lex, d0, d1, d2, d3, out, own, left):
        dense = (d0, d1, d2, d3)
        step = pl.program_id(0)

        def slot_of(x):
            away = (x + 4 - ex_ref[0]) % 4
            return jnp.where(away == 2, 3, jnp.where(away == 3, 1, away * 2))

        def arrange(low, lines):
            for source, c in ((g, core_ref[0]), (other, 1 - core_ref[0])):
                at = pl.multiple_of(c * 4 * part, 4 * part)
                for x in range(4):
                    left[pl.ds(at, 4 * part), x * passages : (x + 1) * passages] = source[
                        :, lines[x], :, low : low + passages
                    ].reshape(4 * part, passages)

        @pl.when(step == 0)
        def _():
            arrange(passages, [slot_of(x) for x in range(4)])

        def finish(total):
            out[...] = total.astype(out.dtype)
            for y in range(4):

                @pl.when(place_ref[0] == y)
                def _():
                    own[...] = total[y * own_rows : (y + 1) * own_rows]

        @pl.when(step < tiles)
        def _():
            finish(matmul(left[...], lex[...].reshape(4 * passages, width), NN))

        @pl.when(step == tiles)
        def _():
            arrange(0, range(4))
            acc = None
            for x in range(4):
                at = slice(x * passages, (x + 1) * passages)
                term = matmul(left[:, at], dense[x][...], NN)
                acc = term if acc is None else acc + term
            finish(acc)

    return pl.pallas_call(
        body,
        out_shape=(
            jax.ShapeDtypeStruct((rows, terms + width), jnp.bfloat16),
            jax.ShapeDtypeStruct((own_rows, terms + width), jnp.float32),
        ),
        grid_spec=pltpu.PrefetchScalarGridSpec(
            num_scalar_prefetch=3,
            grid=(tiles + 1,),
            in_specs=[
                pl.BlockSpec(grads.shape, lambda i, *h: (0, 0, 0, 0)),
                pl.BlockSpec(grads.shape, lambda i, *h: (0, 0, 0, 0)),
                pl.BlockSpec(
                    (4, passages, width), lambda i, *h: (0, 0, jnp.minimum(i, tiles - 1))
                ),
            ]
            + [pl.BlockSpec((passages, width), lambda i, *h: (0, 0))] * 4,
            out_specs=(
                pl.BlockSpec((rows, width), lambda i, *h: (0, i)),
                pl.BlockSpec((own_rows, width), lambda i, *h: (0, i)),
            ),
            scratch_shapes=[pltpu.VMEM((rows, 4 * passages), jnp.bfloat16)],
        ),
        name="query_gradients",
    )(*place, grads, partner, passage_lex, *passage_dense)


def passage_gradients(grads, query_lex, query_dense):
    part, passages = grads.shape[3], grads.shape[4] // 2
    queries, terms = query_lex.shape
    width = query_dense.shape[1]
    tiles = terms // width

    def body(g, ql, qd, out_lex, out_dense, left):
        step = pl.program_id(0)

        def arrange(low):
            blocks = [
                g[:, block // 4, block % 4, :, low : low + passages].reshape(4 * part, passages)
                for block in range(8)
            ]
            left[...] = jnp.concatenate(blocks, axis=0).T

        @pl.when(step == 0)
        def _():
            arrange(passages)

        @pl.when(step == tiles)
        def _():
            arrange(0)

        @pl.when(step < tiles)
        def _():
            out_lex[...] = matmul(left[...], ql[...], NN)

        @pl.when(step == tiles)
        def _():
            out_dense[...] = matmul(left[...], qd[...], NN)

    return pl.pallas_call(
        body,
        grid=(tiles + 1,),
        out_shape=(
            jax.ShapeDtypeStruct((passages, terms), jnp.float32),
            jax.ShapeDtypeStruct((passages, width), jnp.float32),
        ),
        in_specs=[
            pl.BlockSpec(grads.shape, lambda i: (0, 0, 0, 0, 0)),
            pl.BlockSpec((queries, width), lambda i: (0, jnp.minimum(i, tiles - 1))),
            pl.BlockSpec((queries, width), lambda i: (0, 0)),
        ],
        out_specs=(
            pl.BlockSpec((passages, width), lambda i: (0, jnp.minimum(i, tiles - 1))),
            pl.BlockSpec((passages, width), lambda i: (0, 0)),
        ),
        scratch_shapes=[pltpu.VMEM((passages, queries), jnp.bfloat16)],
        name="passage_gradients",
    )(grads, query_lex, query_dense)


def to_line(value, axis):
    return lax.all_to_all(
        jnp.broadcast_to(value[None], (4, *value.shape)), axis, 0, 0, tiled=True
    )


def step(query_lex, query_dense, passage_lex, passage_dense, positives):
    core = lax.axis_index("core")
    zed = lax.axis_index("z")
    ex = lax.axis_index("x")
    queries = query_lex.shape[0]
    local_passages = passage_lex.shape[0]
    rows = queries // 8
    part = rows // 4

    line_lex = lax.all_gather(passage_lex, "x", axis=0)

    def scores_of(half):
        return half_scores(
            half.astype(jnp.int32)[None], query_lex, query_dense, passage_lex, passage_dense
        )

    arrived = lax.ppermute(scores_of(1 - core), "core", [(0, 1), (1, 0)])
    both = arrived + scores_of(core)

    def shifted(value, k):
        return lax.ppermute(value, "x", [(x, (x + k) % 4) for x in range(4)])

    both, passage_later = lax.optimization_barrier((both, passage_dense))
    pieces = lax.all_to_all(both, "z", 0, 0, tiled=True)
    near_dense = [shifted(passage_later, 1), shifted(passage_later, 3)]
    scores4 = pieces.sum(axis=0)
    scores2 = scores4.reshape(rows, 2 * local_passages)
    dense = scores2[:, :local_passages]
    lexical = scores2[:, local_passages:]
    line_scores = [lax.dynamic_index_in_dim(scores4, ex, 0, keepdims=False)]
    for k in (1, 3, 2):
        part_scores = lax.dynamic_index_in_dim(scores4, (ex + k) % 4, 0, keepdims=False)
        line_scores.append(shifted(part_scores, k))

    mine = lax.dynamic_slice(
        positives.reshape(2, 4, 4, part), (core, 0, zed, 0), (1, 4, 1, part)
    ).reshape(rows)
    first_column = lax.axis_index(PLANE) * local_passages
    columns = first_column + lax.broadcasted_iota(jnp.int32, (1, local_passages), 1)
    target = (mine[:, None] == columns).astype(jnp.float32)
    joined = dense + 0.3 * lexical
    scores = (joined, dense, lexical)
    highest = [jnp.max(s, axis=1) for s in scores]
    powers = [jnp.exp(s - h[:, None]) for s, h in zip(scores, highest)]
    stats = (
        highest
        + [jnp.sum(p, axis=1) for p in powers]
        + [
            jnp.sum(powers[0] * (joined - dense), axis=1),
            jnp.sum(powers[0] * (joined - lexical), axis=1),
        ]
        + [jnp.sum(target * s, axis=1) for s in scores]
    )
    stats = jnp.stack(stats)
    stats = lax.all_to_all(
        jnp.broadcast_to(stats[None], (16, *stats.shape)), PLANE, 0, 0, tiled=True
    )
    top = stats[:, 0:3].max(axis=0)
    factor = jnp.exp(stats[:, 0:3] - top[None])
    totals = (stats[:, 3:6] * factor).sum(axis=0)
    weighted = (stats[:, 6:8] * factor[:, 0:1]).sum(axis=0)
    picked = stats[:, 8:11].sum(axis=0)
    logs = top + jnp.log(totals)
    kl_dense = weighted[0] / totals[0] - logs[0] + logs[1]
    kl_lex = weighted[1] / totals[0] - logs[0] + logs[2]
    loss = (
        logs[0]
        - picked[0]
        + 0.5 * (logs[1] - picked[1])
        + 0.5 * (logs[2] - picked[2])
        + 0.5 * kl_dense
        + 0.5 * kl_lex
    )

    def gradients(dense, lexical, logs, target):
        joined = dense + 0.3 * lexical
        prob = [jnp.exp(s - log[..., None]) for s, log in zip((joined, dense, lexical), logs)]
        return jnp.concatenate(
            [
                (0.5 * prob[0] + prob[1] - 1.5 * target).astype(jnp.bfloat16),
                (-0.2 * prob[0] + prob[2] - 0.8 * target).astype(jnp.bfloat16),
            ],
            axis=-1,
        )

    grads = gradients(dense, lexical, logs, target).reshape(4, part, 2 * local_passages)
    line_logs = lax.dynamic_index_in_dim(logs.reshape(3, 4, part), ex, 1, keepdims=False)
    line_mine = lax.dynamic_index_in_dim(mine.reshape(4, part), ex, 0, keepdims=False)
    line_grads = []
    for k, both_scores in zip((0, 1, 3, 2), line_scores):
        start = (lax.axis_index("yh") * 4 + (ex + 4 - k) % 4) * 2 + lax.axis_index("yl")
        line_columns = start * local_passages + lax.broadcasted_iota(
            jnp.int32, (1, local_passages), 1
        )
        line_target = (line_mine[:, None] == line_columns).astype(jnp.float32)
        line_grads.append(
            gradients(
                both_scores[:, :local_passages],
                both_scores[:, local_passages:],
                line_logs,
                line_target,
            )
        )
    line_grads = jnp.stack(line_grads)
    line_grads, passage_far = lax.optimization_barrier((line_grads, passage_dense))
    line_grads = to_line(line_grads, "z")
    far_dense = shifted(passage_far, 2)
    line_dense = [passage_dense, *near_dense, far_dense]
    line_grads, grads = lax.optimization_barrier((line_grads, grads))
    partner_grads = lax.ppermute(line_grads, "core", [(0, 1), (1, 0)])
    own_grads = lax.all_gather(grads, RED, axis=0)
    all_loss = lax.all_gather(loss, RED, axis=0)
    shape = (4, 2, 4, part, 2 * local_passages)
    place = lax.axis_index(COLUMN)

    sums, own = query_gradients(
        [scalar.astype(jnp.int32)[None] for scalar in (place, core, ex)],
        line_grads,
        partner_grads,
        line_lex,
        line_dense,
    )
    sums = lax.all_to_all(sums.reshape(4, 2 * part, -1), COLUMN, 0, 0, tiled=True)
    passage_lex_out, passage_dense_out = passage_gradients(
        own_grads.reshape(shape), query_lex, query_dense
    )

    def summed(low, high):
        total = own[:, low:high]
        for k in range(4):
            total = total + jnp.where(k != place, sums[k, :, low:high].astype(jnp.float32), 0.0)
        return total

    terms = passage_lex.shape[1]
    query_lex_out = summed(0, terms)
    query_dense_out = summed(terms, sums.shape[2])
    ordered = all_loss.reshape(4, 2, 4, part).transpose(1, 2, 0, 3).reshape(queries)
    loss_rows = lax.dynamic_slice_in_dim(ordered, lax.axis_index(RED) * rows, rows)
    return loss_rows, query_lex_out, query_dense_out, passage_lex_out, passage_dense_out


def solution(mesh):
    fine = Mesh(mesh.devices.reshape(2, 4, 4, 2, 2), ("yh", "x", "z", "core", "yl"))
    return jax.shard_map(
        step,
        mesh=fine,
        in_specs=(P(None, RED), P(None, RED), P(PLANE, RED), P(PLANE, RED), P()),
        out_specs=(P(RED), P(PLANE, RED), P(PLANE, RED), P(PLANE, RED), P(PLANE, RED)),
        check_vma=False,
    )
```

```python
import jax
import jax.numpy as jnp
from jax import lax
from jax.experimental import pallas as pl
from jax.experimental.pallas import tpu as pltpu
from jax.sharding import Mesh, PartitionSpec as P

RED = ("z", "core")
PLANE = ("yh", "x", "yl")
COLUMN = ("yh", "yl")
NT = (((1,), (1,)), ((), ()))
NN = (((1,), (0,)), ((), ()))


def matmul(first, second, dims):
    return lax.dot_general(first, second, dims, preferred_element_type=jnp.float32)


def half_scores(half, query_lex, query_dense, passage_lex, passage_dense):
    queries, terms = query_lex.shape
    passages, width = passage_dense.shape
    rows = queries // 8
    part = rows // 4

    def body(half_ref, ql, qd, pl_, pd, out):
        dense = matmul(qd[...], pd[...], NT)
        lexical = matmul(ql[...], pl_[...], NT)
        for x in range(2):
            own = slice(x * rows, (x + 1) * rows)
            out[:, x, :, :passages] = dense[own].reshape(4, part, passages)
            out[:, x, :, passages:] = lexical[own].reshape(4, part, passages)

    return pl.pallas_call(
        body,
        out_shape=jax.ShapeDtypeStruct((4, 4, part, 2 * passages), jnp.float32),
        grid_spec=pltpu.PrefetchScalarGridSpec(
            num_scalar_prefetch=1,
            grid=(2,),
            in_specs=[
                pl.BlockSpec((2 * rows, terms), lambda i, h: (h[0] * 2 + i, 0)),
                pl.BlockSpec((2 * rows, width), lambda i, h: (h[0] * 2 + i, 0)),
                pl.BlockSpec((passages, terms), lambda i, h: (0, 0)),
                pl.BlockSpec((passages, width), lambda i, h: (0, 0)),
            ],
            out_specs=pl.BlockSpec((4, 2, part, 2 * passages), lambda i, h: (0, i, 0, 0)),
        ),
        name="half_scores",
    )(half, query_lex, query_dense, passage_lex, passage_dense)


def query_gradients(place, grads, partner, passage_lex, passage_dense, first, tiles):
    part, passages = grads.shape[2], grads.shape[3] // 2
    width = passages
    steps = tiles + (1 if passage_dense else 0)
    rows, own_rows = 8 * part, 2 * part

    def body(place_ref, core_ref, ex_ref, g, other, lex, *rest):
        *dense, out, own, left = rest
        step = pl.program_id(0)

        def slot_of(x):
            away = (x + 4 - ex_ref[0]) % 4
            return jnp.where(away == 2, 3, jnp.where(away == 3, 1, away * 2))

        def arrange(low, lines):
            for source, c in ((g, core_ref[0]), (other, 1 - core_ref[0])):
                at = pl.multiple_of(c * 4 * part, 4 * part)
                for x in range(4):
                    left[pl.ds(at, 4 * part), x * passages : (x + 1) * passages] = source[
                        :, lines[x], :, low : low + passages
                    ].reshape(4 * part, passages)

        @pl.when(step == 0)
        def _():
            arrange(passages, [slot_of(x) for x in range(4)])

        def finish(total):
            out[...] = total.astype(out.dtype)
            for y in range(4):

                @pl.when(place_ref[0] == y)
                def _():
                    own[...] = total[y * own_rows : (y + 1) * own_rows]

        @pl.when(step < tiles)
        def _():
            finish(matmul(left[...], lex[...].reshape(4 * passages, width), NN))

        if dense:

            @pl.when(step == tiles)
            def _():
                arrange(0, range(4))
                acc = None
                for x in range(4):
                    at = slice(x * passages, (x + 1) * passages)
                    term = matmul(left[:, at], dense[x][...], NN)
                    acc = term if acc is None else acc + term
                finish(acc)

    return pl.pallas_call(
        body,
        out_shape=(
            jax.ShapeDtypeStruct((rows, steps * width), jnp.bfloat16),
            jax.ShapeDtypeStruct((own_rows, steps * width), jnp.float32),
        ),
        grid_spec=pltpu.PrefetchScalarGridSpec(
            num_scalar_prefetch=3,
            grid=(steps,),
            in_specs=[
                pl.BlockSpec(grads.shape, lambda i, *h: (0, 0, 0, 0)),
                pl.BlockSpec(grads.shape, lambda i, *h: (0, 0, 0, 0)),
                pl.BlockSpec(
                    (4, passages, width), lambda i, *h: (0, 0, first + jnp.minimum(i, tiles - 1))
                ),
            ]
            + [pl.BlockSpec((passages, width), lambda i, *h: (0, 0))] * len(passage_dense),
            out_specs=(
                pl.BlockSpec((rows, width), lambda i, *h: (0, i)),
                pl.BlockSpec((own_rows, width), lambda i, *h: (0, i)),
            ),
            scratch_shapes=[pltpu.VMEM((rows, 4 * passages), jnp.bfloat16)],
        ),
        name="query_gradients",
    )(*place, grads, partner, passage_lex, *passage_dense)


def passage_gradients(grads, query_lex, query_dense):
    part, passages = grads.shape[3], grads.shape[4] // 2
    queries, terms = query_lex.shape
    width = query_dense.shape[1]
    tiles = terms // width

    def body(g, ql, qd, out_lex, out_dense, left):
        step = pl.program_id(0)

        def arrange(low):
            blocks = [
                g[:, block // 4, block % 4, :, low : low + passages].reshape(4 * part, passages)
                for block in range(8)
            ]
            left[...] = jnp.concatenate(blocks, axis=0).T

        @pl.when(step == 0)
        def _():
            arrange(passages)

        @pl.when(step == tiles)
        def _():
            arrange(0)

        @pl.when(step < tiles)
        def _():
            out_lex[...] = matmul(left[...], ql[...], NN)

        @pl.when(step == tiles)
        def _():
            out_dense[...] = matmul(left[...], qd[...], NN)

    return pl.pallas_call(
        body,
        grid=(tiles + 1,),
        out_shape=(
            jax.ShapeDtypeStruct((passages, terms), jnp.float32),
            jax.ShapeDtypeStruct((passages, width), jnp.float32),
        ),
        in_specs=[
            pl.BlockSpec(grads.shape, lambda i: (0, 0, 0, 0, 0)),
            pl.BlockSpec((queries, width), lambda i: (0, jnp.minimum(i, tiles - 1))),
            pl.BlockSpec((queries, width), lambda i: (0, 0)),
        ],
        out_specs=(
            pl.BlockSpec((passages, width), lambda i: (0, jnp.minimum(i, tiles - 1))),
            pl.BlockSpec((passages, width), lambda i: (0, 0)),
        ),
        scratch_shapes=[pltpu.VMEM((passages, queries), jnp.bfloat16)],
        name="passage_gradients",
    )(grads, query_lex, query_dense)


def to_line(value, axis):
    return lax.all_to_all(
        jnp.broadcast_to(value[None], (4, *value.shape)), axis, 0, 0, tiled=True
    )


def step(query_lex, query_dense, passage_lex, passage_dense, positives):
    core = lax.axis_index("core")
    zed = lax.axis_index("z")
    ex = lax.axis_index("x")
    queries = query_lex.shape[0]
    local_passages = passage_lex.shape[0]
    rows = queries // 8
    part = rows // 4

    line_lex = lax.all_gather(passage_lex, "x", axis=0)

    def scores_of(half):
        return half_scores(
            half.astype(jnp.int32)[None], query_lex, query_dense, passage_lex, passage_dense
        )

    arrived = lax.ppermute(scores_of(1 - core), "core", [(0, 1), (1, 0)])
    both = arrived + scores_of(core)

    def shifted(value, k):
        return lax.ppermute(value, "x", [(x, (x + k) % 4) for x in range(4)])

    both, passage_later = lax.optimization_barrier((both, passage_dense))
    pieces = lax.all_to_all(both, "z", 0, 0, tiled=True)
    near_dense = [shifted(passage_later, 1), shifted(passage_later, 3)]
    scores4 = pieces.sum(axis=0)
    scores2 = scores4.reshape(rows, 2 * local_passages)
    dense = scores2[:, :local_passages]
    lexical = scores2[:, local_passages:]
    line_scores = [lax.dynamic_index_in_dim(scores4, ex, 0, keepdims=False)]
    for k in (1, 3, 2):
        part_scores = lax.dynamic_index_in_dim(scores4, (ex + k) % 4, 0, keepdims=False)
        line_scores.append(shifted(part_scores, k))

    mine = lax.dynamic_slice(
        positives.reshape(2, 4, 4, part), (core, 0, zed, 0), (1, 4, 1, part)
    ).reshape(rows)
    first_column = lax.axis_index(PLANE) * local_passages
    columns = first_column + lax.broadcasted_iota(jnp.int32, (1, local_passages), 1)
    target = (mine[:, None] == columns).astype(jnp.float32)
    joined = dense + 0.3 * lexical
    scores = (joined, dense, lexical)
    highest = [jnp.max(s, axis=1) for s in scores]
    powers = [jnp.exp(s - h[:, None]) for s, h in zip(scores, highest)]
    stats = (
        highest
        + [jnp.sum(p, axis=1) for p in powers]
        + [
            jnp.sum(powers[0] * (joined - dense), axis=1),
            jnp.sum(powers[0] * (joined - lexical), axis=1),
        ]
        + [jnp.sum(target * s, axis=1) for s in scores]
    )
    stats = jnp.stack(stats)
    stats = lax.all_to_all(
        jnp.broadcast_to(stats[None], (16, *stats.shape)), PLANE, 0, 0, tiled=True
    )
    top = stats[:, 0:3].max(axis=0)
    factor = jnp.exp(stats[:, 0:3] - top[None])
    totals = (stats[:, 3:6] * factor).sum(axis=0)
    weighted = (stats[:, 6:8] * factor[:, 0:1]).sum(axis=0)
    picked = stats[:, 8:11].sum(axis=0)
    logs = top + jnp.log(totals)
    kl_dense = weighted[0] / totals[0] - logs[0] + logs[1]
    kl_lex = weighted[1] / totals[0] - logs[0] + logs[2]
    loss = (
        logs[0]
        - picked[0]
        + 0.5 * (logs[1] - picked[1])
        + 0.5 * (logs[2] - picked[2])
        + 0.5 * kl_dense
        + 0.5 * kl_lex
    )

    def gradients(dense, lexical, logs, target):
        joined = dense + 0.3 * lexical
        prob = [jnp.exp(s - log[..., None]) for s, log in zip((joined, dense, lexical), logs)]
        return jnp.concatenate(
            [
                (0.5 * prob[0] + prob[1] - 1.5 * target).astype(jnp.bfloat16),
                (-0.2 * prob[0] + prob[2] - 0.8 * target).astype(jnp.bfloat16),
            ],
            axis=-1,
        )

    grads = gradients(dense, lexical, logs, target).reshape(4, part, 2 * local_passages)
    line_logs = lax.dynamic_index_in_dim(logs.reshape(3, 4, part), ex, 1, keepdims=False)
    line_mine = lax.dynamic_index_in_dim(mine.reshape(4, part), ex, 0, keepdims=False)
    line_grads = []
    for k, both_scores in zip((0, 1, 3, 2), line_scores):
        start = (lax.axis_index("yh") * 4 + (ex + 4 - k) % 4) * 2 + lax.axis_index("yl")
        line_columns = start * local_passages + lax.broadcasted_iota(
            jnp.int32, (1, local_passages), 1
        )
        line_target = (line_mine[:, None] == line_columns).astype(jnp.float32)
        line_grads.append(
            gradients(
                both_scores[:, :local_passages],
                both_scores[:, local_passages:],
                line_logs,
                line_target,
            )
        )
    line_grads = jnp.stack(line_grads)
    line_grads, passage_far = lax.optimization_barrier((line_grads, passage_dense))
    line_grads = to_line(line_grads, "z")
    far_dense = shifted(passage_far, 2)
    line_dense = [passage_dense, *near_dense, far_dense]
    line_grads, grads = lax.optimization_barrier((line_grads, grads))
    partner_grads = lax.ppermute(line_grads, "core", [(0, 1), (1, 0)])
    own_grads = lax.all_gather(grads, RED, axis=0)
    all_loss = lax.all_gather(loss, RED, axis=0)
    shape = (4, 2, 4, part, 2 * local_passages)
    place = lax.axis_index(COLUMN)

    scalars = [scalar.astype(jnp.int32)[None] for scalar in (place, core, ex)]
    parts = []
    for first, tiles, extra in ((0, 2, []), (2, 2, line_dense)):
        sums, own = query_gradients(
            scalars, line_grads, partner_grads, line_lex, extra, first, tiles
        )
        sums = lax.all_to_all(sums.reshape(4, 2 * part, -1), COLUMN, 0, 0, tiled=True)
        parts.append((sums, own))
    passage_lex_out, passage_dense_out = passage_gradients(
        own_grads.reshape(shape), query_lex, query_dense
    )

    def summed(sums, own, low, high):
        total = own[:, low:high]
        for k in range(4):
            total = total + jnp.where(k != place, sums[k, :, low:high].astype(jnp.float32), 0.0)
        return total

    half = parts[0][1].shape[1]
    query_lex_out = jnp.concatenate(
        [summed(*parts[0], 0, half), summed(*parts[1], 0, half)], axis=1
    )
    query_dense_out = summed(*parts[1], half, half + local_passages)
    ordered = all_loss.reshape(4, 2, 4, part).transpose(1, 2, 0, 3).reshape(queries)
    loss_rows = lax.dynamic_slice_in_dim(ordered, lax.axis_index(RED) * rows, rows)
    return loss_rows, query_lex_out, query_dense_out, passage_lex_out, passage_dense_out


def solution(mesh):
    fine = Mesh(mesh.devices.reshape(2, 4, 4, 2, 2), ("yh", "x", "z", "core", "yl"))
    return jax.shard_map(
        step,
        mesh=fine,
        in_specs=(P(None, RED), P(None, RED), P(PLANE, RED), P(PLANE, RED), P()),
        out_specs=(P(RED), P(PLANE, RED), P(PLANE, RED), P(PLANE, RED), P(PLANE, RED)),
        check_vma=False,
    )
```
